256 devices in a mesh: prow: 32 (over x, y, core), pcol: 8 (over z).
Axes of the slice: x: 4, y: 4, z: 8, core: 2. Of those that a mesh axis runs over, the one named last changes fastest.
Arguments:
- right_zero: bfloat16 [32, 8, 1, 512, 512], P('prow', 'pcol'), may hold values from -6 to 6
- inverse_zero: bfloat16 [32, 8, 1, 512, 512], P('prow', 'pcol'), as said below
- factor_blocks: bfloat16 [32, 8, 6, 512, 512], P('prow', 'pcol'), may hold values from -0.046875 to 0.046875
- block_rows: int32 [32, 8, 6], P('prow', 'pcol'), may hold values from 0 to 3, as said below
- block_cols: int32 [32, 8, 6], P('prow', 'pcol'), may hold values from 0 to 7
- block_count: int32 [32, 8], P('prow', 'pcol'), may hold values from 1 to 6, as said below
- right_one: bfloat16 [8, 4, 512, 512], P('pcol'), may hold values from -6 to 6
- inverse_one: bfloat16 [8, 4, 512, 512], P('pcol'), as said below
Outputs:
- solved_zero: bfloat16 [32, 8, 1, 512, 512], P('prow', 'pcol')
- solved_one: bfloat16 [8, 4, 512, 512], P('pcol')
The draws below stay inside these ranges and needn't reach their ends.
Inputs may be any that keep to these rules, and one draw needn't show every extreme that they name: `block_count`: some grid position uses exactly 6 blocks. Among the first block_count entries of a grid position, the pairs (block_rows, block_cols) are distinct. `inverse_zero`: each [512, 512] matrix is lower triangular with a positive diagonal. `inverse_one`: each [512, 512] matrix is lower triangular with a positive diagonal.
All inputs are finite; a program needn't handle non-finite values.
Results may differ from the reference program's by a relative error of at most 0.0053.
Values may be sent and summed in bfloat16 or wider, within the bound.
A program may use at most 64 MiB of HBM per device.

```python
import math
import jax
import jax.numpy as jnp
from jax import lax

W = 512
R = 512
NBLK = 6
K0 = 1
M1 = 4
N_PROW = 32
N_PCOL = 8


def triangle(key, leading):
    full_shape = tuple(leading) + (W, W)
    row_ids = lax.broadcasted_iota(jnp.int32, full_shape, len(full_shape) - 2)
    col_ids = lax.broadcasted_iota(jnp.int32, full_shape, len(full_shape) - 1)
    diagonal = jnp.exp(jax.random.uniform(jax.random.fold_in(key, 1), full_shape, jnp.float32, math.log(0.7), math.log(1.4)))
    lower_part = jax.random.normal(jax.random.fold_in(key, 2), full_shape, jnp.float32) * (0.5 / math.sqrt(W))
    result = jnp.where(row_ids == col_ids, diagonal, jnp.where(col_ids < row_ids, lower_part, 0.0))
    return result.astype(jnp.bfloat16)


def draw_inverse_zero(key, part):
    return triangle(jax.random.fold_in(key, 41), (N_PROW, N_PCOL, K0))


def draw_inverse_one(key, part):
    return triangle(jax.random.fold_in(key, 43), (N_PCOL, M1))


def pair_draw(key):
    device_keys = jax.random.split(jax.random.fold_in(key, 17), N_PROW * N_PCOL)
    ordering = jax.vmap(lambda k: jax.random.permutation(k, M1 * N_PCOL * K0)[:NBLK])(device_keys)
    return ordering.reshape(N_PROW, N_PCOL, NBLK).astype(jnp.int32)


def draw_block_rows(key, part):
    return (pair_draw(key) // (N_PCOL * K0)).astype(jnp.int32)


def draw_block_cols(key, part):
    return (pair_draw(key) % (N_PCOL * K0)).astype(jnp.int32)


def draw_block_count(key, part):
    spread = jax.random.randint(jax.random.fold_in(key, 23), (N_PROW, N_PCOL), 0, NBLK)
    counts = 1 + spread * spread // NBLK
    chosen = jax.random.randint(jax.random.fold_in(key, 29), (), 0, N_PROW * N_PCOL)
    flat_ids = lax.broadcasted_iota(jnp.int32, (N_PROW, N_PCOL), 0) * N_PCOL + lax.broadcasted_iota(jnp.int32, (N_PROW, N_PCOL), 1)
    return jnp.where(flat_ids == chosen, NBLK, counts).astype(jnp.int32)


def level_of(key, shape, cuts, least, largest):
    factor_of, own = 1.0, jax.random.fold_in(key, 6)
    for dim, parts in cuts:
        heights = jnp.exp(jax.random.uniform(jax.random.fold_in(own, dim), (parts,), jnp.float32, least / len(cuts), largest / len(cuts)))
        factor_of = factor_of * jnp.repeat(heights, shape[dim] // parts).reshape([-1 if axis == dim else 1 for axis in range(len(shape))])
    return factor_of


def normal_values(own_key, dims, deviation, most, pieces=(), held_as=jnp.bfloat16):
    drawn = jax.random.normal(own_key, dims, jnp.float32) * deviation
    if len(pieces) > 0:
        drawn = level_of(own_key, dims, pieces, -0.22, 0.18) * drawn
    return jnp.clip(drawn, min=-most, max=most).astype(held_as)


def setup_inputs(seed: int = 0) -> dict:
    streams_of = jax.random.split(jax.random.key(seed), 9)
    return {
        "right_zero": normal_values(streams_of[0], (N_PROW, N_PCOL, K0, W, R), 1.0, 6.0, ((0, 32), (1, 8))),
        "inverse_zero": draw_inverse_zero(jax.random.fold_in(streams_of[8], 71), 0),
        "factor_blocks": normal_values(streams_of[2], (N_PROW, N_PCOL, NBLK, W, W), (W * 32) ** -0.5, 0.046875, ((0, 32), (1, 8))),
        "block_rows": draw_block_rows(jax.random.fold_in(streams_of[8], 71), 0),
        "block_cols": draw_block_cols(jax.random.fold_in(streams_of[8], 71), 0),
        "block_count": draw_block_count(jax.random.fold_in(streams_of[8], 71), 0),
        "right_one": normal_values(streams_of[6], (N_PCOL, M1, W, R), 1.0, 6.0, ((0, 8),)),
        "inverse_one": draw_inverse_one(jax.random.fold_in(streams_of[8], 71), 0),
    }


def reference(right_zero, inverse_zero, factor_blocks, block_rows, block_cols, block_count, right_one, inverse_one):
    solved_zero = jnp.einsum("rckij,rckjn->rckin", inverse_zero.astype(jnp.float32), right_zero.astype(jnp.float32)).astype(jnp.bfloat16)
    panels = solved_zero.reshape(N_PROW, N_PCOL * K0, W, R)

    def column_update(c):
        def over_rows(r, running):
            def over_blocks(b, carry_sum):
                target = block_rows[r, c, b]
                source = block_cols[r, c, b]
                product = jnp.dot(factor_blocks[r, c, b], panels[r, source], preferred_element_type=jnp.float32)
                return carry_sum.at[target].add(product)
            return lax.fori_loop(0, block_count[r, c], over_blocks, running)
        return lax.fori_loop(0, N_PROW, over_rows, jnp.zeros((M1, W, R), jnp.float32))

    update = lax.map(column_update, jnp.arange(N_PCOL, dtype=jnp.int32))
    residual = (right_one.astype(jnp.float32) - update).astype(jnp.bfloat16)
    solved_one = jnp.einsum("cmij,cmjn->cmin", inverse_one.astype(jnp.float32), residual.astype(jnp.float32)).astype(jnp.bfloat16)
    return (solved_zero, solved_one)
```

```python
import functools

import jax
import jax.numpy as jnp
from jax import lax
from jax.experimental import pallas as pl
from jax.experimental.pallas import tpu as pltpu
from jax.sharding import PartitionSpec as P

MESH = pl.DeviceIdType.MESH
BF = jnp.bfloat16
F32 = jnp.float32
W = 512
CW = 128
NCH = 4
NZ = 8
CHIPS = 16
OWN = 64
HALF = 1024


def fused(
    rows_s, cols_s, count_s, inv_hbm, right_hbm, blocks_hbm, right_one_hbm,
    res_out, own_out,
    inv_v, right_v, blocks_v, ro_v, acc,
    p0, p1, p2, p3,
    pair_send, pair_recv, rs_send, rs_recv, res_v,
    load_sem, out_sem, z_send, z_recv, pair_ssem, pair_rsem, rs_ssem, rs_rsem, ag_ssem, ag_rsem,
    sib_ssem, sib_rsem,
):
    panels = (p0, p1, p2, p3)
    r = lax.axis_index("prow")
    z = lax.axis_index("pcol")
    core = lax.rem(r, 2)
    chip = r // 2
    up = lax.rem(z + 1, NZ)
    down = lax.rem(z + NZ - 1, NZ)
    sibling = chip * 2 + 1 - core

    def peer(j):
        return lax.rem(chip + j, CHIPS) * 2 + core

    cp_inv = pltpu.make_async_copy(inv_hbm, inv_v, load_sem.at[0])
    cp_right = pltpu.make_async_copy(right_hbm, right_v, load_sem.at[1])
    cp_inv.start()
    cp_right.start()

    barrier = pltpu.get_barrier_semaphore()
    for zz in (up, down):
        pl.semaphore_signal(barrier, inc=1, device_id=(r, zz), device_id_type=MESH)
    pl.semaphore_signal(barrier, inc=1, device_id=(sibling, z), device_id_type=MESH)

    def greet(j, carry):
        pl.semaphore_signal(barrier, inc=1, device_id=(peer(j), z), device_id_type=MESH)
        return carry

    lax.fori_loop(1, CHIPS, greet, 0)

    cp_blocks = pltpu.make_async_copy(blocks_hbm, blocks_v, load_sem.at[2])
    cp_blocks.start()
    my_rows = pl.multiple_of(lax.rem(chip, 8) * OWN, OWN)
    cp_ro = pltpu.make_async_copy(
        right_one_hbm.at[core * 2 + chip // 8, pl.ds(my_rows, OWN), :], ro_v, load_sem.at[3]
    )
    cp_ro.start()

    def own_panel(k):
        panels[k][z] = jnp.dot(
            inv_v[...], right_v[:, k * CW:(k + 1) * CW], preferred_element_type=F32
        ).astype(BF)

    def z_copy(k, way, half, d):
        origin = lax.rem(z - d + NZ, NZ) if way == 0 else lax.rem(z + d, NZ)
        piece = panels[k].at[origin, pl.ds(half * 256, 256), :]
        return pltpu.make_async_remote_copy(
            src_ref=piece,
            dst_ref=piece,
            send_sem=z_send.at[k],
            recv_sem=z_recv.at[k, way, half, d],
            device_id=(r, up if way == 0 else down),
            device_id_type=MESH,
        )

    def z_arrive(k, way, half, d):
        origin = lax.rem(z - d - 1 + NZ, NZ) if way == 0 else lax.rem(z + d + 1, NZ)
        piece = panels[k].at[origin, pl.ds(half * 256, 256), :]
        pltpu.make_async_copy(piece, piece, z_recv.at[k, way, half, d]).wait()

    def z_step(k, d):
        order = ((0, 0), (1, 1), (0, 1), (1, 0)) if d < 3 else ((0, 0), (1, 1))
        for way, half in order:
            if d > 0:
                z_arrive(k, way, half, d - 1)
            z_copy(k, way, half, d).start()

    def z_final(k):
        z_arrive(k, 0, 1, 2)
        z_arrive(k, 1, 0, 2)
        z_arrive(k, 0, 0, 3)
        z_arrive(k, 1, 1, 3)

    def pair_copy(k):
        return pltpu.make_async_remote_copy(
            src_ref=pair_send.at[k], dst_ref=pair_recv.at[k],
            send_sem=pair_ssem.at[k], recv_sem=pair_rsem.at[k],
            device_id=(sibling, z), device_id_type=MESH,
        )

    def stage_a(k):
        acc[...] = jnp.zeros_like(acc)

        def block(b, carry):
            product = jnp.dot(blocks_v[b], panels[k][cols_s[b]], preferred_element_type=F32)
            used = b < count_s[0]
            for m in range(4):
                weight = jnp.where(jnp.logical_and(used, rows_s[b] == m), 1.0, 0.0)
                acc[m] += product * weight
            return carry

        lax.fori_loop(0, 6, block, 0)
        away = 2 - core * 2
        for i in range(2):
            pair_send[k, i * W:(i + 1) * W, :] = acc[away + i].astype(BF)
        pair_copy(k).start()

    def rs_copy(k, j):
        target = lax.rem(chip + j, CHIPS)
        return pltpu.make_async_remote_copy(
            src_ref=rs_send.at[k, pl.ds(pl.multiple_of(target * OWN, OWN), OWN), :],
            dst_ref=rs_recv.at[k, j - 1],
            send_sem=rs_ssem.at[k], recv_sem=rs_rsem.at[k],
            device_id=(peer(j), z), device_id_type=MESH,
        )

    def stage_b(k):
        pair_copy(k).wait()
        for i in range(2):
            both = acc[core * 2 + i] + pair_recv[k, i * W:(i + 1) * W, :].astype(F32)
            rs_send[k, i * W:(i + 1) * W, :] = both.astype(BF)

        def send(j, carry):
            rs_copy(k, j).start()
            return carry

        lax.fori_loop(1, CHIPS, send, 0)

    def own_rows():
        return pl.ds(pl.multiple_of(core * HALF + chip * OWN, OWN), OWN)

    def ag_copy(k, j):
        piece = res_v.at[k, own_rows(), :]
        return pltpu.make_async_remote_copy(
            src_ref=piece, dst_ref=piece,
            send_sem=ag_ssem.at[k], recv_sem=ag_rsem.at[k],
            device_id=(peer(j), z), device_id_type=MESH,
        )

    def all_bytes(k, sem):
        return pltpu.make_async_copy(rs_recv.at[k], rs_recv.at[k], sem.at[k])

    def stage_c(k):
        all_bytes(k, rs_rsem).wait()
        total = rs_send[k, pl.ds(pl.multiple_of(chip * OWN, OWN), OWN), :].astype(F32)
        for j in range(CHIPS - 1):
            total += rs_recv[k, j].astype(F32)
        left = ro_v[:, k * CW:(k + 1) * CW].astype(F32) - total
        res_v[k, own_rows(), :] = left.astype(BF)

        def send(j, carry):
            ag_copy(k, j).start()
            return carry

        lax.fori_loop(1, CHIPS, send, 0)

    def sib_copy(k):
        piece = res_v.at[k, pl.ds(pl.multiple_of(core * HALF, HALF), HALF), :]
        return pltpu.make_async_remote_copy(
            src_ref=piece, dst_ref=piece,
            send_sem=sib_ssem.at[k], recv_sem=sib_rsem.at[k],
            device_id=(sibling, z), device_id_type=MESH,
        )

    def stage_d(k):
        all_bytes(k, ag_rsem).wait()
        sib_copy(k).start()

    def out_copy(k):
        return pltpu.make_async_copy(res_v.at[k], res_out.at[k], out_sem.at[k])

    def own_copy(k):
        return pltpu.make_async_copy(panels[k].at[z], own_out.at[k], out_sem.at[NCH + k])

    def stage_e(k):
        sib_copy(k).wait()
        out_copy(k).start()

    cp_inv.wait()
    cp_right.wait()
    own_panel(0)
    pl.semaphore_wait(barrier, CHIPS + 2)
    z_step(0, 0)
    for k in range(1, NCH):
        own_panel(k)
    cp_blocks.wait()
    cp_ro.wait()
    for k in range(NCH):
        own_copy(k).start()

    z_step(0, 1)
    z_step(0, 2)
    z_step(1, 0)
    z_step(0, 3)
    z_final(0)

    z_step(1, 1)
    stage_a(0)
    z_step(1, 2)
    stage_b(0)
    z_step(2, 0)
    z_step(1, 3)
    z_final(1)

    z_step(2, 1)
    stage_a(1)
    stage_c(0)
    z_step(2, 2)
    stage_b(1)
    stage_d(0)
    z_step(3, 0)
    z_step(2, 3)
    z_final(2)

    z_step(3, 1)
    stage_e(0)
    stage_a(2)
    stage_c(1)
    z_step(3, 2)
    stage_b(2)
    stage_d(1)
    z_step(3, 3)
    stage_c(2)
    z_final(3)

    stage_e(1)
    stage_a(3)
    stage_b(3)
    stage_d(2)
    stage_c(3)
    stage_e(2)
    stage_d(3)
    stage_e(3)

    for k in range(NCH):
        piece = panels[k].at[0:7]
        pltpu.make_async_copy(piece, piece, z_send.at[k]).wait()
        all_bytes(k, rs_ssem).wait()
        all_bytes(k, ag_ssem).wait()
        out_copy(k).wait()
        own_copy(k).wait()


def finish(inv_ref, res_ref, own_ref, one_ref, zero_ref):
    for c in range(NCH):
        one_ref[0, :, c * CW:(c + 1) * CW] = jnp.dot(
            inv_ref[0], res_ref[c], preferred_element_type=F32
        ).astype(BF)
    zero_ref[...] = own_ref[0]


def body(
    right_zero, inverse_zero, factor_blocks, block_rows, block_cols, block_count, right_one, inverse_one,
):
    smem = pl.BlockSpec(memory_space=pltpu.SMEM)
    hbm = pl.BlockSpec(memory_space=pl.ANY)
    dma = pltpu.SemaphoreType.DMA
    res, own = pl.pallas_call(
        fused,
        out_shape=(
            jax.ShapeDtypeStruct((NCH, 4 * W, CW), BF),
            jax.ShapeDtypeStruct((NCH, W, CW), BF),
        ),
        in_specs=[smem, smem, smem, hbm, hbm, hbm, hbm],
        out_specs=(hbm, hbm),
        scratch_shapes=[
            pltpu.VMEM((W, W), BF),
            pltpu.VMEM((W, W), BF),
            pltpu.VMEM((6, W, W), BF),
            pltpu.VMEM((OWN, W), BF),
            pltpu.VMEM((4, W, CW), F32),
        ]
        + [pltpu.VMEM((NZ, W, CW), BF)] * NCH
        + [
            pltpu.VMEM((NCH, HALF, CW), BF),
            pltpu.VMEM((NCH, HALF, CW), BF),
            pltpu.VMEM((NCH, HALF, CW), BF),
            pltpu.VMEM((NCH, CHIPS - 1, OWN, CW), BF),
            pltpu.VMEM((NCH, 4 * W, CW), BF),
            dma((4,)),
            dma((2 * NCH,)),
            dma((NCH,)),
            dma((NCH, 2, 2, 4)),
            dma((NCH,)), dma((NCH,)),
            dma((NCH,)), dma((NCH,)),
            dma((NCH,)), dma((NCH,)),
            dma((NCH,)), dma((NCH,)),
        ],
        compiler_params=pltpu.CompilerParams(
            collective_id=0, has_side_effects=True, vmem_limit_bytes=40 * 1024 * 1024
        ),
    )(
        block_rows[0, 0], block_cols[0, 0], block_count[0],
        inverse_zero[0, 0, 0], right_zero[0, 0, 0], factor_blocks[0, 0], right_one[0],
    )
    one, zero = pl.pallas_call(
        finish,
        grid=(4,),
        out_shape=(
            jax.ShapeDtypeStruct((4, W, W), BF),
            jax.ShapeDtypeStruct((W, W), BF),
        ),
        in_specs=[
            pl.BlockSpec((1, W, W), lambda m: (m, 0, 0)),
            pl.BlockSpec((NCH, W, CW), lambda m: (0, m, 0)),
            pl.BlockSpec((1, W, CW), lambda m: (m, 0, 0)),
        ],
        out_specs=(
            pl.BlockSpec((1, W, W), lambda m: (m, 0, 0)),
            pl.BlockSpec((W, CW), lambda m: (0, m)),
        ),
    )(inverse_one[0], res, own)
    return (zero[None, None, None], one[None])


def solution(mesh):
    in_specs = (
        P("prow", "pcol", None, None, None),
        P("prow", "pcol", None, None, None),
        P("prow", "pcol", None, None, None),
        P("prow", "pcol", None),
        P("prow", "pcol", None),
        P("prow", "pcol"),
        P("pcol", None, None, None),
        P("pcol", None, None, None),
    )
    out_specs = (P("prow", "pcol", None, None, None), P("pcol", None, None, None))
    return jax.shard_map(body, mesh=mesh, in_specs=in_specs, out_specs=out_specs, check_vma=False)
```

```python
import functools

import jax
import jax.numpy as jnp
from jax import lax
from jax.experimental import pallas as pl
from jax.experimental.pallas import tpu as pltpu
from jax.sharding import PartitionSpec as P

MESH = pl.DeviceIdType.MESH
BF = jnp.bfloat16
F32 = jnp.float32
W = 512
CW = 128
NCH = 4
NZ = 8
CHIPS = 16
OWN = 64
HALF = 1024


def fused(
    rows_s, cols_s, count_s, inv_hbm, right_hbm, blocks_hbm, right_one_hbm, inv_one_hbm,
    one_out, own_out,
    inv_v, right_v, blocks_v, ro_v, inv_one_v, one_v, own_v, acc,
    p0, p1, p2, p3,
    pair_send, pair_recv, rs_send, rs_recv, res_v,
    load_sem, out_sem, z_send, z_recv, pair_ssem, pair_rsem, rs_ssem, rs_rsem, ag_ssem, ag_rsem,
    sib_ssem, sib_rsem,
):
    panels = (p0, p1, p2, p3)
    r = lax.axis_index("prow")
    z = lax.axis_index("pcol")
    core = lax.rem(r, 2)
    chip = r // 2
    up = lax.rem(z + 1, NZ)
    down = lax.rem(z + NZ - 1, NZ)
    sibling = chip * 2 + 1 - core

    def peer(j):
        return lax.rem(chip + j, CHIPS) * 2 + core

    cp_inv = pltpu.make_async_copy(inv_hbm, inv_v, load_sem.at[0])
    cp_right = pltpu.make_async_copy(right_hbm, right_v, load_sem.at[1])
    cp_inv.start()
    cp_right.start()

    barrier = pltpu.get_barrier_semaphore()
    for zz in (up, down):
        pl.semaphore_signal(barrier, inc=1, device_id=(r, zz), device_id_type=MESH)
    pl.semaphore_signal(barrier, inc=1, device_id=(sibling, z), device_id_type=MESH)

    def greet(j, carry):
        pl.semaphore_signal(barrier, inc=1, device_id=(peer(j), z), device_id_type=MESH)
        return carry

    lax.fori_loop(1, CHIPS, greet, 0)

    cp_blocks = pltpu.make_async_copy(blocks_hbm, blocks_v, load_sem.at[2])
    cp_blocks.start()
    my_rows = pl.multiple_of(core * 256 + lax.rem(chip, 4) * OWN, OWN)
    cp_ro = pltpu.make_async_copy(
        right_one_hbm.at[chip // 4, pl.ds(my_rows, OWN), :], ro_v, load_sem.at[3]
    )
    cp_ro.start()
    cp_inv_one = pltpu.make_async_copy(inv_one_hbm, inv_one_v, load_sem.at[4])
    cp_inv_one.start()

    def own_panel(k):
        x = right_v[:, k * CW:(k + 1) * CW]
        top = jnp.dot(inv_v[:256, :256], x[:256], preferred_element_type=F32).astype(BF)
        low = jnp.dot(inv_v[256:, :], x, preferred_element_type=F32).astype(BF)
        panels[k][z, :256] = top
        panels[k][z, 256:] = low
        own_v[:256, k * CW:(k + 1) * CW] = top
        own_v[256:, k * CW:(k + 1) * CW] = low

    def z_copy(k, way, half, d):
        origin = lax.rem(z - d + NZ, NZ) if way == 0 else lax.rem(z + d, NZ)
        piece = panels[k].at[origin, pl.ds(half * 128, 128), :]
        return pltpu.make_async_remote_copy(
            src_ref=piece,
            dst_ref=piece,
            send_sem=z_send.at[k],
            recv_sem=z_recv.at[k, way, half, d],
            device_id=(r, up if way == 0 else down),
            device_id_type=MESH,
        )

    def z_arrive(k, way, half, d):
        origin = lax.rem(z - d - 1 + NZ, NZ) if way == 0 else lax.rem(z + d + 1, NZ)
        piece = panels[k].at[origin, pl.ds(half * 128, 128), :]
        pltpu.make_async_copy(piece, piece, z_recv.at[k, way, half, d]).wait()

    def z_step(k, d):
        for i in range(4):
            for way in range(2):
                part = (i + 2 * way) % 4
                far = (part < 2) if way == 0 else (part >= 2)
                if d < 3 or far:
                    if d > 0:
                        z_arrive(k, way, part, d - 1)
                    z_copy(k, way, part, d).start()

    def z_final(k):
        for part in range(4):
            for way in range(2):
                far = (part < 2) if way == 0 else (part >= 2)
                z_arrive(k, way, part, 3 if far else 2)

    def pair_copy(k):
        return pltpu.make_async_remote_copy(
            src_ref=pair_send.at[k], dst_ref=pair_recv.at[k],
            send_sem=pair_ssem.at[k], recv_sem=pair_rsem.at[k],
            device_id=(sibling, z), device_id_type=MESH,
        )

    def products(k, side):
        rows = pl.ds(pl.multiple_of(side * 256, 256), 256)
        acc[side] = jnp.zeros((4, 256, CW), F32)

        def block(b, carry):
            product = jnp.dot(blocks_v[b, rows, :], panels[k][cols_s[b]], preferred_element_type=F32)
            used = b < count_s[0]
            for m in range(4):
                weight = jnp.where(jnp.logical_and(used, rows_s[b] == m), 1.0, 0.0)
                acc[side, m] += product * weight
            return carry

        lax.fori_loop(0, 6, block, 0)

    def stage_a(k):
        products(k, 1 - core)
        for m in range(4):
            pair_send[k, m * 256:(m + 1) * 256, :] = acc[1 - core, m].astype(BF)
        pair_copy(k).start()
        products(k, core)

    def rs_copy(k, j):
        target = lax.rem(chip + j, CHIPS)
        return pltpu.make_async_remote_copy(
            src_ref=rs_send.at[k, pl.ds(pl.multiple_of(target * OWN, OWN), OWN), :],
            dst_ref=rs_recv.at[k, j - 1],
            send_sem=rs_ssem.at[k], recv_sem=rs_rsem.at[k],
            device_id=(peer(j), z), device_id_type=MESH,
        )

    def stage_b(k):
        pair_copy(k).wait()
        for m in range(4):
            both = acc[core, m] + pair_recv[k, m * 256:(m + 1) * 256, :].astype(F32)
            rs_send[k, m * 256:(m + 1) * 256, :] = both.astype(BF)

        def send(j, carry):
            rs_copy(k, j).start()
            return carry

        lax.fori_loop(1, CHIPS, send, 0)

    def own_rows():
        return pl.ds(pl.multiple_of(core * HALF + chip * OWN, OWN), OWN)

    def ag_copy(k, j):
        piece = res_v.at[k, own_rows(), :]
        return pltpu.make_async_remote_copy(
            src_ref=piece, dst_ref=piece,
            send_sem=ag_ssem.at[k], recv_sem=ag_rsem.at[k],
            device_id=(peer(j), z), device_id_type=MESH,
        )

    def all_bytes(k, sem):
        return pltpu.make_async_copy(rs_recv.at[k], rs_recv.at[k], sem.at[k])

    def stage_c(k):
        all_bytes(k, rs_rsem).wait()
        total = rs_send[k, pl.ds(pl.multiple_of(chip * OWN, OWN), OWN), :].astype(F32)
        for j in range(CHIPS - 1):
            total += rs_recv[k, j].astype(F32)
        left = ro_v[:, k * CW:(k + 1) * CW].astype(F32) - total
        res_v[k, own_rows(), :] = left.astype(BF)

        def send(j, carry):
            ag_copy(k, j).start()
            return carry

        lax.fori_loop(1, CHIPS, send, 0)

    def sib_copy(k):
        piece = res_v.at[k, pl.ds(pl.multiple_of(core * HALF, HALF), HALF), :]
        return pltpu.make_async_remote_copy(
            src_ref=piece, dst_ref=piece,
            send_sem=sib_ssem.at[k], recv_sem=sib_rsem.at[k],
            device_id=(sibling, z), device_id_type=MESH,
        )

    def stage_d(k):
        all_bytes(k, ag_rsem).wait()
        sib_copy(k).start()

    def out_copy(k):
        cols = pl.ds(k * CW, CW)
        return pltpu.make_async_copy(one_v.at[:, :, cols], one_out.at[:, :, cols], out_sem.at[k])

    cp_own = pltpu.make_async_copy(own_v, own_out, out_sem.at[NCH])

    def stage_e(k):
        sib_copy(k).wait()
        cols = slice(k * CW, (k + 1) * CW)
        for m in range(4):
            top = res_v[k, m * 256:(m + 1) * 256, :]
            low = res_v[k, HALF + m * 256:HALF + (m + 1) * 256, :]
            one_v[m, :256, cols] = jnp.dot(
                inv_one_v[m, :256, :256], top, preferred_element_type=F32
            ).astype(BF)
            one_v[m, 256:, cols] = (
                jnp.dot(inv_one_v[m, 256:, :256], top, preferred_element_type=F32)
                + jnp.dot(inv_one_v[m, 256:, 256:], low, preferred_element_type=F32)
            ).astype(BF)
        out_copy(k).start()

    cp_inv.wait()
    cp_right.wait()
    own_panel(0)
    pl.semaphore_wait(barrier, CHIPS + 2)
    z_step(0, 0)
    own_panel(1)
    z_step(1, 0)
    own_panel(2)
    own_panel(3)
    cp_own.start()
    cp_blocks.wait()
    cp_ro.wait()
    cp_inv_one.wait()
    z_step(0, 1)
    z_step(0, 2)
    z_step(0, 3)
    z_step(1, 1)
    z_final(0)
    stage_a(0)
    z_step(2, 0)
    z_step(1, 2)
    stage_b(0)
    z_step(1, 3)
    stage_c(0)
    z_step(2, 1)
    z_final(1)
    stage_a(1)
    stage_d(0)
    z_step(3, 0)
    z_step(2, 2)
    stage_b(1)
    stage_e(0)
    z_step(2, 3)
    stage_c(1)
    z_step(3, 1)
    z_final(2)
    stage_a(2)
    stage_d(1)
    z_step(3, 2)
    stage_b(2)
    stage_e(1)
    z_step(3, 3)
    stage_c(2)
    z_final(3)
    stage_a(3)
    stage_d(2)
    stage_b(3)
    stage_e(2)
    stage_c(3)
    stage_d(3)
    stage_e(3)

    for k in range(NCH):
        piece = panels[k].at[0:7]
        pltpu.make_async_copy(piece, piece, z_send.at[k]).wait()
        all_bytes(k, rs_ssem).wait()
        all_bytes(k, ag_ssem).wait()
        out_copy(k).wait()
    cp_own.wait()


def body(
    right_zero, inverse_zero, factor_blocks, block_rows, block_cols, block_count, right_one, inverse_one,
):
    smem = pl.BlockSpec(memory_space=pltpu.SMEM)
    hbm = pl.BlockSpec(memory_space=pl.ANY)
    dma = pltpu.SemaphoreType.DMA
    one, zero = pl.pallas_call(
        fused,
        out_shape=(
            jax.ShapeDtypeStruct((4, W, W), BF),
            jax.ShapeDtypeStruct((W, W), BF),
        ),
        in_specs=[smem, smem, smem, hbm, hbm, hbm, hbm, hbm],
        out_specs=(hbm, hbm),
        scratch_shapes=[
            pltpu.VMEM((W, W), BF),
            pltpu.VMEM((W, W), BF),
            pltpu.VMEM((6, W, W), BF),
            pltpu.VMEM((OWN, W), BF),
            pltpu.VMEM((4, W, W), BF),
            pltpu.VMEM((4, W, W), BF),
            pltpu.VMEM((W, W), BF),
            pltpu.VMEM((2, 4, 256, CW), F32),
        ]
        + [pltpu.VMEM((NZ, W, CW), BF)] * NCH
        + [
            pltpu.VMEM((NCH, HALF, CW), BF),
            pltpu.VMEM((NCH, HALF, CW), BF),
            pltpu.VMEM((NCH, HALF, CW), BF),
            pltpu.VMEM((NCH, CHIPS - 1, OWN, CW), BF),
            pltpu.VMEM((NCH, 4 * W, CW), BF),
            dma((5,)),
            dma((NCH + 1,)),
            dma((NCH,)),
            dma((NCH, 2, 4, 4)),
            dma((NCH,)), dma((NCH,)),
            dma((NCH,)), dma((NCH,)),
            dma((NCH,)), dma((NCH,)),
            dma((NCH,)), dma((NCH,)),
        ],
        compiler_params=pltpu.CompilerParams(
            collective_id=0, has_side_effects=True, vmem_limit_bytes=60 * 1024 * 1024
        ),
    )(
        block_rows[0, 0], block_cols[0, 0], block_count[0],
        inverse_zero[0, 0, 0], right_zero[0, 0, 0], factor_blocks[0, 0], right_one[0], inverse_one[0],
    )
    return (zero[None, None, None], one[None])


def solution(mesh):
    in_specs = (
        P("prow", "pcol", None, None, None),
        P("prow", "pcol", None, None, None),
        P("prow", "pcol", None, None, None),
        P("prow", "pcol", None),
        P("prow", "pcol", None),
        P("prow", "pcol"),
        P("pcol", None, None, None),
        P("pcol", None, None, None),
    )
    out_specs = (P("prow", "pcol", None, None, None), P("pcol", None, None, None))
    return jax.shard_map(body, mesh=mesh, in_specs=in_specs, out_specs=out_specs, check_vma=False)
```

```python
import functools

import jax
import jax.numpy as jnp
from jax import lax
from jax.experimental import pallas as pl
from jax.experimental.pallas import tpu as pltpu
from jax.sharding import PartitionSpec as P

MESH = pl.DeviceIdType.MESH
BF = jnp.bfloat16
F32 = jnp.float32
W = 512
CW = 128
NCH = 4
NZ = 8
CHIPS = 16
OWN = 64
HALF = 1024
FAR_FIRST = (10, 6, 14, 9, 11, 2, 8, 5, 7, 13, 15, 1, 3, 4, 12)


def fused(
    rows_hbm, cols_hbm, count_hbm, inv_hbm, right_hbm, blocks_hbm, right_one_hbm, inv_one_hbm,
    one_out, own_out,
    rows_s, cols_s, count_s, inv_v, right_v, blocks_v, ro_v, inv_one_v, one_v, own_v, acc,
    p0, p1, p2, p3,
    pair_send, pair_recv, rs_send, rs_recv, res_v,
    load_sem, out_sem, z_send, z_recv, pair_ssem, pair_rsem, rs_ssem, rs_rsem, ag_ssem, ag_rsem,
    sib_ssem, sib_rsem,
):
    panels = (p0, p1, p2, p3)
    r = lax.axis_index("prow")
    z = lax.axis_index("pcol")
    core = lax.rem(r, 2)
    chip = r // 2
    up = lax.rem(z + 1, NZ)
    down = lax.rem(z + NZ - 1, NZ)
    sibling = chip * 2 + 1 - core

    cx = chip // 4
    cy = lax.rem(chip, 4)

    def chip_at(j):
        return lax.rem(cx + j // 4, 4) * 4 + lax.rem(cy + j % 4, 4)

    def peer(j):
        return chip_at(j) * 2 + core

    cp_inv = pltpu.make_async_copy(inv_hbm, inv_v, load_sem.at[0])
    cp_right = pltpu.make_async_copy(right_hbm, right_v, load_sem.at[1])
    cp_inv.start()
    cp_right.start()

    barrier = pltpu.get_barrier_semaphore()
    for zz in (up, down):
        pl.semaphore_signal(barrier, inc=1, device_id=(r, zz), device_id_type=MESH)
    pl.semaphore_signal(barrier, inc=1, device_id=(sibling, z), device_id_type=MESH)

    for j in FAR_FIRST:
        pl.semaphore_signal(barrier, inc=1, device_id=(peer(j), z), device_id_type=MESH)

    cp_blocks = pltpu.make_async_copy(blocks_hbm, blocks_v, load_sem.at[2])
    cp_blocks.start()
    my_rows = pl.multiple_of(core * 256 + lax.rem(chip, 4) * OWN, OWN)
    cp_ro = pltpu.make_async_copy(
        right_one_hbm.at[chip // 4, pl.ds(my_rows, OWN), :], ro_v, load_sem.at[3]
    )
    cp_ro.start()
    cp_inv_one = pltpu.make_async_copy(inv_one_hbm, inv_one_v, load_sem.at[4])
    cp_inv_one.start()
    lists = [
        pltpu.make_async_copy(src, dst, load_sem.at[5 + i])
        for i, (src, dst) in enumerate(((rows_hbm, rows_s), (cols_hbm, cols_s), (count_hbm, count_s)))
    ]
    for copy in lists:
        copy.start()

    def own_panel(k):
        x = right_v[:, k * CW:(k + 1) * CW]
        top = jnp.dot(inv_v[:256, :256], x[:256], preferred_element_type=F32).astype(BF)
        low = jnp.dot(inv_v[256:, :], x, preferred_element_type=F32).astype(BF)
        panels[k][z, :256] = top
        panels[k][z, 256:] = low
        own_v[:256, k * CW:(k + 1) * CW] = top
        own_v[256:, k * CW:(k + 1) * CW] = low

    def z_copy(k, way, half, d):
        origin = lax.rem(z - d + NZ, NZ) if way == 0 else lax.rem(z + d, NZ)
        piece = panels[k].at[origin, pl.ds(half * 128, 128), :]
        return pltpu.make_async_remote_copy(
            src_ref=piece,
            dst_ref=piece,
            send_sem=z_send.at[k],
            recv_sem=z_recv.at[k, way, half, d],
            device_id=(r, up if way == 0 else down),
            device_id_type=MESH,
        )

    def z_arrive(k, way, half, d):
        origin = lax.rem(z - d - 1 + NZ, NZ) if way == 0 else lax.rem(z + d + 1, NZ)
        piece = panels[k].at[origin, pl.ds(half * 128, 128), :]
        pltpu.make_async_copy(piece, piece, z_recv.at[k, way, half, d]).wait()

    def z_pass(k, way, part, d):
        if d > 0:
            z_arrive(k, way, part, d - 1)
        z_copy(k, way, part, d).start()

    def z_step(k, d):
        steps = []
        for i in range(4):
            for way in range(2):
                part = (i + 2 * way) % 4
                far = (part < 2) if way == 0 else (part >= 2)
                if d < 3 or far:
                    steps.append(functools.partial(z_pass, k, way, part, d))
        return steps

    def z_final(k):
        for part in range(4):
            for way in range(2):
                far = (part < 2) if way == 0 else (part >= 2)
                z_arrive(k, way, part, 3 if far else 2)

    def pair_copy(k):
        return pltpu.make_async_remote_copy(
            src_ref=pair_send.at[k], dst_ref=pair_recv.at[k],
            send_sem=pair_ssem.at[k], recv_sem=pair_rsem.at[k],
            device_id=(sibling, z), device_id_type=MESH,
        )

    def product(k, side, b):
        rows = pl.ds(pl.multiple_of(side * 256, 256), 256)
        value = jnp.dot(blocks_v[b, rows, :], panels[k][cols_s[b]], preferred_element_type=F32)
        used = b < count_s[0]
        for m in range(4):
            weight = jnp.where(jnp.logical_and(used, rows_s[b] == m), 1.0, 0.0)
            if b == 0:
                acc[side, m] = value * weight
            else:
                acc[side, m] += value * weight

    def send_away(k):
        for m in range(4):
            pair_send[k, m * 256:(m + 1) * 256, :] = acc[1 - core, m].astype(BF)
        pair_copy(k).start()

    def stage_a(k):
        away = [functools.partial(product, k, 1 - core, b) for b in range(6)]
        keep = [functools.partial(product, k, core, b) for b in range(6)]
        return away + [functools.partial(send_away, k)] + keep

    def rs_copy(k, j):
        target = chip_at(j)
        return pltpu.make_async_remote_copy(
            src_ref=rs_send.at[k, pl.ds(pl.multiple_of(target * OWN, OWN), OWN), :],
            dst_ref=rs_recv.at[k, j - 1],
            send_sem=rs_ssem.at[k], recv_sem=rs_rsem.at[k],
            device_id=(peer(j), z), device_id_type=MESH,
        )

    def stage_b(k):
        pair_copy(k).wait()
        for m in range(4):
            both = acc[core, m] + pair_recv[k, m * 256:(m + 1) * 256, :].astype(F32)
            rs_send[k, m * 256:(m + 1) * 256, :] = both.astype(BF)

        for j in FAR_FIRST:
            rs_copy(k, j).start()

    def own_rows():
        return pl.ds(pl.multiple_of(core * HALF + chip * OWN, OWN), OWN)

    def ag_copy(k, j):
        piece = res_v.at[k, own_rows(), :]
        return pltpu.make_async_remote_copy(
            src_ref=piece, dst_ref=piece,
            send_sem=ag_ssem.at[k], recv_sem=ag_rsem.at[k],
            device_id=(peer(j), z), device_id_type=MESH,
        )

    def all_bytes(k, sem):
        return pltpu.make_async_copy(rs_recv.at[k], rs_recv.at[k], sem.at[k])

    def stage_c(k):
        all_bytes(k, rs_rsem).wait()
        total = rs_send[k, pl.ds(pl.multiple_of(chip * OWN, OWN), OWN), :].astype(F32)
        for j in range(CHIPS - 1):
            total += rs_recv[k, j].astype(F32)
        left = ro_v[:, k * CW:(k + 1) * CW].astype(F32) - total
        res_v[k, own_rows(), :] = left.astype(BF)

        for j in FAR_FIRST:
            ag_copy(k, j).start()

    def sib_copy(k):
        piece = res_v.at[k, pl.ds(pl.multiple_of(core * HALF, HALF), HALF), :]
        return pltpu.make_async_remote_copy(
            src_ref=piece, dst_ref=piece,
            send_sem=sib_ssem.at[k], recv_sem=sib_rsem.at[k],
            device_id=(sibling, z), device_id_type=MESH,
        )

    def stage_d(k):
        all_bytes(k, ag_rsem).wait()
        sib_copy(k).start()

    def out_copy(k):
        cols = pl.ds(k * CW, CW)
        return pltpu.make_async_copy(one_v.at[:, :, cols], one_out.at[:, :, cols], out_sem.at[k])

    cp_own = pltpu.make_async_copy(own_v, own_out, out_sem.at[NCH])

    def stage_e(k):
        sib_copy(k).wait()
        cols = slice(k * CW, (k + 1) * CW)
        for m in range(4):
            top = res_v[k, m * 256:(m + 1) * 256, :]
            low = res_v[k, HALF + m * 256:HALF + (m + 1) * 256, :]
            one_v[m, :256, cols] = jnp.dot(
                inv_one_v[m, :256, :256], top, preferred_element_type=F32
            ).astype(BF)
            one_v[m, 256:, cols] = (
                jnp.dot(inv_one_v[m, 256:, :256], top, preferred_element_type=F32)
                + jnp.dot(inv_one_v[m, 256:, 256:], low, preferred_element_type=F32)
            ).astype(BF)
        out_copy(k).start()

    cp_inv.wait()
    cp_right.wait()
    own_panel(0)
    pl.semaphore_wait(barrier, CHIPS + 2)
    def loaded():
        cp_own.start()
        cp_blocks.wait()
        for copy in lists:
            copy.wait()
        cp_ro.wait()
        cp_inv_one.wait()

    schedule = (
        (z_step(0, 0),),
        ([functools.partial(own_panel, 1)],),
        (z_step(1, 0),),
        ([functools.partial(own_panel, 2)],),
        ([functools.partial(own_panel, 3)],),
        ([loaded],),
        (z_step(0, 1),),
        (z_step(1, 1),),
        (z_step(0, 2),),
        (z_step(0, 3),),
        (z_step(2, 0),),
        (z_step(1, 2),),
        ([functools.partial(z_final, 0)],),
        (stage_a(0),),
        (z_step(2, 1),),
        ([functools.partial(stage_b, 0)],),
        (z_step(1, 3),),
        (z_step(2, 2),),
        (z_step(3, 0),),
        ([functools.partial(z_final, 1)],),
        (stage_a(1),),
        (z_step(2, 3),),
        ([functools.partial(stage_c, 0)],),
        ([functools.partial(stage_b, 1)],),
        (z_step(3, 1),),
        ([functools.partial(z_final, 2)],),
        (stage_a(2), z_step(3, 2),),
        ([functools.partial(stage_d, 0)],),
        ([functools.partial(stage_b, 2)],),
        ([functools.partial(stage_c, 1)],),
        (z_step(3, 3),),
        ([functools.partial(stage_e, 0)],),
        ([functools.partial(stage_d, 1)],),
        ([functools.partial(z_final, 3)],),
        (stage_a(3),),
        ([functools.partial(stage_b, 3)],),
        ([functools.partial(stage_c, 2)],),
        ([functools.partial(stage_e, 1)],),
        ([functools.partial(stage_c, 3)],),
        ([functools.partial(stage_d, 2)],),
        ([functools.partial(stage_e, 2)],),
        ([functools.partial(stage_d, 3)],),
        ([functools.partial(stage_e, 3)],),
    )
    for phase in schedule:
        longest = max(len(steps) for steps in phase)
        for i in range(longest):
            for steps in phase:
                for step in steps[i * len(steps) // longest:(i + 1) * len(steps) // longest]:
                    step()

    for k in range(NCH):
        piece = panels[k].at[0:7]
        pltpu.make_async_copy(piece, piece, z_send.at[k]).wait()
        all_bytes(k, rs_ssem).wait()
        all_bytes(k, ag_ssem).wait()
        out_copy(k).wait()
    cp_own.wait()


def body(
    right_zero, inverse_zero, factor_blocks, block_rows, block_cols, block_count, right_one, inverse_one,
):
    hbm = pl.BlockSpec(memory_space=pl.ANY)
    dma = pltpu.SemaphoreType.DMA
    one, zero = pl.pallas_call(
        fused,
        out_shape=(
            jax.ShapeDtypeStruct((4, W, W), BF),
            jax.ShapeDtypeStruct((W, W), BF),
        ),
        in_specs=[hbm, hbm, hbm, hbm, hbm, hbm, hbm, hbm],
        out_specs=(hbm, hbm),
        scratch_shapes=[
            pltpu.SMEM((6,), jnp.int32),
            pltpu.SMEM((6,), jnp.int32),
            pltpu.SMEM((1,), jnp.int32),
            pltpu.VMEM((W, W), BF),
            pltpu.VMEM((W, W), BF),
            pltpu.VMEM((6, W, W), BF),
            pltpu.VMEM((OWN, W), BF),
            pltpu.VMEM((4, W, W), BF),
            pltpu.VMEM((4, W, W), BF),
            pltpu.VMEM((W, W), BF),
            pltpu.VMEM((2, 4, 256, CW), F32),
        ]
        + [pltpu.VMEM((NZ, W, CW), BF)] * NCH
        + [
            pltpu.VMEM((NCH, HALF, CW), BF),
            pltpu.VMEM((NCH, HALF, CW), BF),
            pltpu.VMEM((NCH, HALF, CW), BF),
            pltpu.VMEM((NCH, CHIPS - 1, OWN, CW), BF),
            pltpu.VMEM((NCH, 4 * W, CW), BF),
            dma((8,)),
            dma((NCH + 1,)),
            dma((NCH,)),
            dma((NCH, 2, 4, 4)),
            dma((NCH,)), dma((NCH,)),
            dma((NCH,)), dma((NCH,)),
            dma((NCH,)), dma((NCH,)),
            dma((NCH,)), dma((NCH,)),
        ],
        compiler_params=pltpu.CompilerParams(
            collective_id=0, has_side_effects=True, vmem_limit_bytes=40 * 1024 * 1024
        ),
    )(
        block_rows[0, 0], block_cols[0, 0], block_count[0],
        *(
            pltpu.with_memory_space_constraint(operand, pltpu.HBM)
            for operand in (
                inverse_zero[0, 0, 0], right_zero[0, 0, 0],
                factor_blocks[0, 0], right_one[0], inverse_one[0],
            )
        ),
    )
    return (zero[None, None, None], one[None])


def solution(mesh):
    in_specs = (
        P("prow", "pcol", None, None, None),
        P("prow", "pcol", None, None, None),
        P("prow", "pcol", None, None, None),
        P("prow", "pcol", None),
        P("prow", "pcol", None),
        P("prow", "pcol"),
        P("pcol", None, None, None),
        P("pcol", None, None, None),
    )
    out_specs = (P("prow", "pcol", None, None, None), P("pcol", None, None, None))
    return jax.shard_map(body, mesh=mesh, in_specs=in_specs, out_specs=out_specs, check_vma=False)
```

```python
import functools

import jax
import jax.numpy as jnp
from jax import lax
from jax.experimental import pallas as pl
from jax.experimental.pallas import tpu as pltpu
from jax.sharding import PartitionSpec as P

MESH = pl.DeviceIdType.MESH
BF = jnp.bfloat16
F32 = jnp.float32
W = 512
CW = 128
NCH = 4
NZ = 8
CHIPS = 16
OWN = 64
HALF = 1024
FAR_FIRST = (10, 6, 14, 9, 11, 2, 8, 5, 7, 13, 15, 1, 3, 4, 12)


def fused(
    rows_hbm, cols_hbm, count_hbm, inv_hbm, right_hbm, blocks_hbm, right_one_hbm, inv_one_hbm,
    one_v, own_v,
    rows_s, cols_s, count_s, inv_v, right_v, blocks_v, ro_v, inv_one_v, acc,
    p0, p1, p2, p3,
    pair_send, pair_recv, rs_send, rs_recv, res_v,
    load_sem, z_send, z_recv, pair_ssem, pair_rsem, rs_ssem, rs_rsem, ag_ssem, ag_rsem,
    sib_ssem, sib_rsem,
):
    panels = (p0, p1, p2, p3)
    r = lax.axis_index("prow")
    z = lax.axis_index("pcol")
    core = lax.rem(r, 2)
    chip = r // 2
    up = lax.rem(z + 1, NZ)
    down = lax.rem(z + NZ - 1, NZ)
    sibling = chip * 2 + 1 - core

    cx = chip // 4
    cy = lax.rem(chip, 4)

    def chip_at(j):
        return lax.rem(cx + j // 4, 4) * 4 + lax.rem(cy + j % 4, 4)

    def peer(j):
        return chip_at(j) * 2 + core

    cp_inv = pltpu.make_async_copy(inv_hbm, inv_v, load_sem.at[0])
    cp_right = pltpu.make_async_copy(right_hbm, right_v, load_sem.at[1])
    cp_inv.start()
    cp_right.start()

    barrier = pltpu.get_barrier_semaphore()
    for zz in (up, down):
        pl.semaphore_signal(barrier, inc=1, device_id=(r, zz), device_id_type=MESH)
    pl.semaphore_signal(barrier, inc=1, device_id=(sibling, z), device_id_type=MESH)

    for j in FAR_FIRST:
        pl.semaphore_signal(barrier, inc=1, device_id=(peer(j), z), device_id_type=MESH)

    cp_blocks = pltpu.make_async_copy(blocks_hbm, blocks_v, load_sem.at[2])
    cp_blocks.start()
    my_rows = pl.multiple_of(core * 256 + lax.rem(chip, 4) * OWN, OWN)
    cp_ro = pltpu.make_async_copy(
        right_one_hbm.at[chip // 4, pl.ds(my_rows, OWN), :], ro_v, load_sem.at[3]
    )
    cp_ro.start()
    cp_inv_one = pltpu.make_async_copy(inv_one_hbm, inv_one_v, load_sem.at[4])
    cp_inv_one.start()
    lists = [
        pltpu.make_async_copy(src, dst, load_sem.at[5 + i])
        for i, (src, dst) in enumerate(((rows_hbm, rows_s), (cols_hbm, cols_s), (count_hbm, count_s)))
    ]
    for copy in lists:
        copy.start()

    def own_panel(k):
        x = right_v[:, k * CW:(k + 1) * CW]
        top = jnp.dot(inv_v[:256, :256], x[:256], preferred_element_type=F32).astype(BF)
        low = jnp.dot(inv_v[256:, :], x, preferred_element_type=F32).astype(BF)
        panels[k][z, :256] = top
        panels[k][z, 256:] = low
        own_v[:256, k * CW:(k + 1) * CW] = top
        own_v[256:, k * CW:(k + 1) * CW] = low

    def z_copy(k, way, half, d):
        origin = lax.rem(z - d + NZ, NZ) if way == 0 else lax.rem(z + d, NZ)
        piece = panels[k].at[origin, pl.ds(half * 128, 128), :]
        return pltpu.make_async_remote_copy(
            src_ref=piece,
            dst_ref=piece,
            send_sem=z_send.at[k],
            recv_sem=z_recv.at[k, way, half, d],
            device_id=(r, up if way == 0 else down),
            device_id_type=MESH,
        )

    def z_arrive(k, way, half, d):
        origin = lax.rem(z - d - 1 + NZ, NZ) if way == 0 else lax.rem(z + d + 1, NZ)
        piece = panels[k].at[origin, pl.ds(half * 128, 128), :]
        pltpu.make_async_copy(piece, piece, z_recv.at[k, way, half, d]).wait()

    def z_pass(k, way, part, d):
        if d > 0:
            z_arrive(k, way, part, d - 1)
        z_copy(k, way, part, d).start()

    def z_step(k, d):
        steps = []
        for i in range(4):
            for way in range(2):
                part = (i + 2 * way) % 4
                far = (part < 2) if way == 0 else (part >= 2)
                if d < 3 or far:
                    steps.append(functools.partial(z_pass, k, way, part, d))
        return steps

    def z_final(k):
        for part in range(4):
            for way in range(2):
                far = (part < 2) if way == 0 else (part >= 2)
                z_arrive(k, way, part, 3 if far else 2)

    def pair_copy(k):
        return pltpu.make_async_remote_copy(
            src_ref=pair_send.at[k], dst_ref=pair_recv.at[k],
            send_sem=pair_ssem.at[k], recv_sem=pair_rsem.at[k],
            device_id=(sibling, z), device_id_type=MESH,
        )

    def product(k, side, b):
        rows = pl.ds(pl.multiple_of(side * 256, 256), 256)
        value = jnp.dot(blocks_v[b, rows, :], panels[k][cols_s[b]], preferred_element_type=F32)
        used = b < count_s[0]
        for m in range(4):
            weight = jnp.where(jnp.logical_and(used, rows_s[b] == m), 1.0, 0.0)
            if b == 0:
                acc[side, m] = value * weight
            else:
                acc[side, m] += value * weight

    def send_away(k):
        for m in range(4):
            pair_send[k, m * 256:(m + 1) * 256, :] = acc[1 - core, m].astype(BF)
        pair_copy(k).start()

    def stage_a(k):
        away = [functools.partial(product, k, 1 - core, b) for b in range(6)]
        keep = [functools.partial(product, k, core, b) for b in range(6)]
        return away + [functools.partial(send_away, k)] + keep

    def rs_copy(k, j):
        target = chip_at(j)
        return pltpu.make_async_remote_copy(
            src_ref=rs_send.at[k, pl.ds(pl.multiple_of(target * OWN, OWN), OWN), :],
            dst_ref=rs_recv.at[k, j - 1],
            send_sem=rs_ssem.at[k], recv_sem=rs_rsem.at[k],
            device_id=(peer(j), z), device_id_type=MESH,
        )

    def stage_b(k):
        pair_copy(k).wait()
        for m in range(4):
            both = acc[core, m] + pair_recv[k, m * 256:(m + 1) * 256, :].astype(F32)
            rs_send[k, m * 256:(m + 1) * 256, :] = both.astype(BF)

        for j in FAR_FIRST:
            rs_copy(k, j).start()

    def own_rows():
        return pl.ds(pl.multiple_of(core * HALF + chip * OWN, OWN), OWN)

    def ag_copy(k, j):
        piece = res_v.at[k, own_rows(), :]
        return pltpu.make_async_remote_copy(
            src_ref=piece, dst_ref=piece,
            send_sem=ag_ssem.at[k], recv_sem=ag_rsem.at[k],
            device_id=(peer(j), z), device_id_type=MESH,
        )

    def all_bytes(k, sem):
        return pltpu.make_async_copy(rs_recv.at[k], rs_recv.at[k], sem.at[k])

    def stage_c(k):
        all_bytes(k, rs_rsem).wait()
        total = rs_send[k, pl.ds(pl.multiple_of(chip * OWN, OWN), OWN), :].astype(F32)
        for j in range(CHIPS - 1):
            total += rs_recv[k, j].astype(F32)
        left = ro_v[:, k * CW:(k + 1) * CW].astype(F32) - total
        res_v[k, own_rows(), :] = left.astype(BF)

        for j in FAR_FIRST:
            ag_copy(k, j).start()

    def sib_copy(k):
        piece = res_v.at[k, pl.ds(pl.multiple_of(core * HALF, HALF), HALF), :]
        return pltpu.make_async_remote_copy(
            src_ref=piece, dst_ref=piece,
            send_sem=sib_ssem.at[k], recv_sem=sib_rsem.at[k],
            device_id=(sibling, z), device_id_type=MESH,
        )

    def stage_d(k):
        all_bytes(k, ag_rsem).wait()
        sib_copy(k).start()

    def stage_e(k):
        sib_copy(k).wait()
        cols = slice(k * CW, (k + 1) * CW)
        for m in range(4):
            top = res_v[k, m * 256:(m + 1) * 256, :]
            low = res_v[k, HALF + m * 256:HALF + (m + 1) * 256, :]
            one_v[m, :256, cols] = jnp.dot(
                inv_one_v[m, :256, :256], top, preferred_element_type=F32
            ).astype(BF)
            one_v[m, 256:, cols] = (
                jnp.dot(inv_one_v[m, 256:, :256], top, preferred_element_type=F32)
                + jnp.dot(inv_one_v[m, 256:, 256:], low, preferred_element_type=F32)
            ).astype(BF)

    cp_inv.wait()
    cp_right.wait()
    own_panel(0)
    pl.semaphore_wait(barrier, CHIPS + 2)
    def loaded():
        cp_blocks.wait()
        for copy in lists:
            copy.wait()
        cp_ro.wait()
        cp_inv_one.wait()

    schedule = (
        (z_step(0, 0),),
        ([functools.partial(own_panel, 1)],),
        (z_step(1, 0),),
        ([functools.partial(own_panel, 2)],),
        ([functools.partial(own_panel, 3)],),
        ([loaded],),
        (z_step(0, 1),),
        (z_step(1, 1),),
        (z_step(0, 2),),
        (z_step(0, 3),),
        (z_step(2, 0),),
        (z_step(1, 2),),
        ([functools.partial(z_final, 0)],),
        (stage_a(0),),
        (z_step(2, 1),),
        ([functools.partial(stage_b, 0)],),
        (z_step(1, 3),),
        (z_step(2, 2),),
        (z_step(3, 0),),
        ([functools.partial(z_final, 1)],),
        (stage_a(1),),
        (z_step(2, 3),),
        ([functools.partial(stage_c, 0)],),
        ([functools.partial(stage_b, 1)],),
        (z_step(3, 1),),
        ([functools.partial(z_final, 2)],),
        (stage_a(2), z_step(3, 2),),
        ([functools.partial(stage_d, 0)],),
        ([functools.partial(stage_b, 2)],),
        ([functools.partial(stage_c, 1)],),
        (z_step(3, 3),),
        ([functools.partial(stage_e, 0)],),
        ([functools.partial(stage_d, 1)],),
        ([functools.partial(z_final, 3)],),
        (stage_a(3),),
        ([functools.partial(stage_b, 3)],),
        ([functools.partial(stage_c, 2)],),
        ([functools.partial(stage_e, 1)],),
        ([functools.partial(stage_c, 3)],),
        ([functools.partial(stage_d, 2)],),
        ([functools.partial(stage_e, 2)],),
        ([functools.partial(stage_d, 3)],),
        ([functools.partial(stage_e, 3)],),
    )
    for phase in schedule:
        longest = max(len(steps) for steps in phase)
        for i in range(longest):
            for steps in phase:
                for step in steps[i * len(steps) // longest:(i + 1) * len(steps) // longest]:
                    step()

    for k in range(NCH):
        piece = panels[k].at[0:7]
        pltpu.make_async_copy(piece, piece, z_send.at[k]).wait()
        all_bytes(k, rs_ssem).wait()
        all_bytes(k, ag_ssem).wait()


def body(
    right_zero, inverse_zero, factor_blocks, block_rows, block_cols, block_count, right_one, inverse_one,
):
    hbm = pl.BlockSpec(memory_space=pl.ANY)
    vm = pl.BlockSpec(memory_space=pltpu.VMEM)
    dma = pltpu.SemaphoreType.DMA
    one, zero = pl.pallas_call(
        fused,
        out_shape=(
            jax.ShapeDtypeStruct((4, W, W), BF),
            jax.ShapeDtypeStruct((W, W), BF),
        ),
        in_specs=[hbm, hbm, hbm, hbm, hbm, hbm, hbm, hbm],
        out_specs=(vm, vm),
        scratch_shapes=[
            pltpu.SMEM((6,), jnp.int32),
            pltpu.SMEM((6,), jnp.int32),
            pltpu.SMEM((1,), jnp.int32),
            pltpu.VMEM((W, W), BF),
            pltpu.VMEM((W, W), BF),
            pltpu.VMEM((6, W, W), BF),
            pltpu.VMEM((OWN, W), BF),
            pltpu.VMEM((4, W, W), BF),
            pltpu.VMEM((2, 4, 256, CW), F32),
        ]
        + [pltpu.VMEM((NZ, W, CW), BF)] * NCH
        + [
            pltpu.VMEM((NCH, HALF, CW), BF),
            pltpu.VMEM((NCH, HALF, CW), BF),
            pltpu.VMEM((NCH, HALF, CW), BF),
            pltpu.VMEM((NCH, CHIPS - 1, OWN, CW), BF),
            pltpu.VMEM((NCH, 4 * W, CW), BF),
            dma((8,)),
            dma((NCH,)),
            dma((NCH, 2, 4, 4)),
            dma((NCH,)), dma((NCH,)),
            dma((NCH,)), dma((NCH,)),
            dma((NCH,)), dma((NCH,)),
            dma((NCH,)), dma((NCH,)),
        ],
        compiler_params=pltpu.CompilerParams(
            collective_id=0, has_side_effects=True, vmem_limit_bytes=40 * 1024 * 1024
        ),
    )(
        pltpu.with_memory_space_constraint(block_rows[0, 0], pltpu.HBM),
        pltpu.with_memory_space_constraint(block_cols[0, 0], pltpu.HBM),
        block_count[0],
        *(
            pltpu.with_memory_space_constraint(operand, pltpu.HBM)
            for operand in (
                inverse_zero[0, 0, 0], right_zero[0, 0, 0],
                factor_blocks[0, 0], right_one[0], inverse_one[0],
            )
        ),
    )
    return (zero[None, None, None], one[None])


def solution(mesh):
    in_specs = (
        P("prow", "pcol", None, None, None),
        P("prow", "pcol", None, None, None),
        P("prow", "pcol", None, None, None),
        P("prow", "pcol", None),
        P("prow", "pcol", None),
        P("prow", "pcol"),
        P("pcol", None, None, None),
        P("pcol", None, None, None),
    )
    out_specs = (P("prow", "pcol", None, None, None), P("pcol", None, None, None))
    return jax.shard_map(body, mesh=mesh, in_specs=in_specs, out_specs=out_specs, check_vma=False)
```

```python
import functools

import jax
import jax.numpy as jnp
from jax import lax
from jax.experimental import pallas as pl
from jax.experimental.pallas import tpu as pltpu
from jax.sharding import PartitionSpec as P

MESH = pl.DeviceIdType.MESH
BF = jnp.bfloat16
F32 = jnp.float32
W = 512
CW = 128
NCH = 4
NZ = 8
CHIPS = 16
OWN = 64
HALF = 1024
FAR_FIRST = (10, 6, 14, 9, 11, 2, 8, 5, 7, 13, 15, 1, 3, 4, 12)


def fused(
    rows_hbm, cols_hbm, count_hbm, inv_hbm, right_hbm, blocks_hbm, right_one_hbm, inv_one_hbm,
    one_v, own_v,
    rows_s, cols_s, count_s, inv_v, right_v, blocks_v, ro_v, inv_one_v, acc,
    p0, p1, p2, p3,
    pair_send, pair_recv, rs_send, rs_recv, res_v,
    load_sem, z_send, z_recv, pair_ssem, pair_rsem, rs_ssem, rs_rsem, ag_ssem, ag_rsem,
    sib_ssem, sib_rsem,
):
    panels = (p0, p1, p2, p3)
    r = lax.axis_index("prow")
    z = lax.axis_index("pcol")
    core = lax.rem(r, 2)
    chip = r // 2
    up = lax.rem(z + 1, NZ)
    down = lax.rem(z + NZ - 1, NZ)
    sibling = chip * 2 + 1 - core

    cx = chip // 4
    cy = lax.rem(chip, 4)

    def chip_at(j):
        return lax.rem(cx + j // 4, 4) * 4 + lax.rem(cy + j % 4, 4)

    def peer(j):
        return chip_at(j) * 2 + core

    cp_inv = pltpu.make_async_copy(inv_hbm, inv_v, load_sem.at[0])
    cp_right = pltpu.make_async_copy(right_hbm, right_v, load_sem.at[1])
    cp_inv.start()
    cp_right.start()

    barrier = pltpu.get_barrier_semaphore()
    for zz in (up, down):
        pl.semaphore_signal(barrier, inc=1, device_id=(r, zz), device_id_type=MESH)
    pl.semaphore_signal(barrier, inc=1, device_id=(sibling, z), device_id_type=MESH)

    for j in FAR_FIRST:
        pl.semaphore_signal(barrier, inc=1, device_id=(peer(j), z), device_id_type=MESH)

    cp_blocks = pltpu.make_async_copy(blocks_hbm, blocks_v, load_sem.at[2])
    cp_blocks.start()
    my_rows = pl.multiple_of(core * 256 + lax.rem(chip, 4) * OWN, OWN)
    cp_ro = pltpu.make_async_copy(
        right_one_hbm.at[chip // 4, pl.ds(my_rows, OWN), :], ro_v, load_sem.at[3]
    )
    cp_ro.start()
    cp_inv_one = pltpu.make_async_copy(inv_one_hbm, inv_one_v, load_sem.at[4])
    cp_inv_one.start()
    lists = [
        pltpu.make_async_copy(src, dst, load_sem.at[5 + i])
        for i, (src, dst) in enumerate(((rows_hbm, rows_s), (cols_hbm, cols_s), (count_hbm, count_s)))
    ]
    for copy in lists:
        copy.start()

    def own_panel(k):
        x = right_v[:, k * CW:(k + 1) * CW]
        top = jnp.dot(inv_v[:256, :256], x[:256], preferred_element_type=F32).astype(BF)
        low = jnp.dot(inv_v[256:, :], x, preferred_element_type=F32).astype(BF)
        panels[k][z, :256] = top
        panels[k][z, 256:] = low
        own_v[:256, k * CW:(k + 1) * CW] = top
        own_v[256:, k * CW:(k + 1) * CW] = low

    def z_copy(k, way, half, d):
        origin = lax.rem(z - d + NZ, NZ) if way == 0 else lax.rem(z + d, NZ)
        piece = panels[k].at[origin, pl.ds(half * 128, 128), :]
        return pltpu.make_async_remote_copy(
            src_ref=piece,
            dst_ref=piece,
            send_sem=z_send.at[k],
            recv_sem=z_recv.at[k, way, half, d],
            device_id=(r, up if way == 0 else down),
            device_id_type=MESH,
        )

    def z_arrive(k, way, half, d):
        origin = lax.rem(z - d - 1 + NZ, NZ) if way == 0 else lax.rem(z + d + 1, NZ)
        piece = panels[k].at[origin, pl.ds(half * 128, 128), :]
        pltpu.make_async_copy(piece, piece, z_recv.at[k, way, half, d]).wait()

    def z_pass(k, way, part, d):
        if d > 0:
            z_arrive(k, way, part, d - 1)
        z_copy(k, way, part, d).start()

    def z_step(k, d):
        steps = []
        for i in range(4):
            for way in range(2):
                part = (i + 2 * way) % 4
                far = (part < 2) if way == 0 else (part >= 2)
                if d < 3 or far:
                    steps.append(functools.partial(z_pass, k, way, part, d))
        return steps

    def z_final(k):
        for part in range(4):
            for way in range(2):
                far = (part < 2) if way == 0 else (part >= 2)
                z_arrive(k, way, part, 3 if far else 2)

    def pair_copy(k):
        return pltpu.make_async_remote_copy(
            src_ref=pair_send.at[k], dst_ref=pair_recv.at[k],
            send_sem=pair_ssem.at[k], recv_sem=pair_rsem.at[k],
            device_id=(sibling, z), device_id_type=MESH,
        )

    def product(k, side, b):
        rows = pl.ds(pl.multiple_of(side * 256, 256), 256)
        value = jnp.dot(blocks_v[b, rows, :], panels[k][cols_s[b]], preferred_element_type=F32)
        used = b < count_s[0]
        for m in range(4):
            weight = jnp.where(jnp.logical_and(used, rows_s[b] == m), 1.0, 0.0)
            if b == 0:
                acc[side, m] = value * weight
            else:
                acc[side, m] += value * weight

    def send_away(k):
        for m in range(4):
            pair_send[k, m * 256:(m + 1) * 256, :] = acc[1 - core, m].astype(BF)
        pair_copy(k).start()

    def stage_a(k):
        away = [functools.partial(product, k, 1 - core, b) for b in range(6)]
        keep = [functools.partial(product, k, core, b) for b in range(6)]
        return away + [functools.partial(send_away, k)] + keep

    def rs_copy(k, j):
        target = chip_at(j)
        return pltpu.make_async_remote_copy(
            src_ref=rs_send.at[k, pl.ds(pl.multiple_of(target * OWN, OWN), OWN), :],
            dst_ref=rs_recv.at[k, j - 1],
            send_sem=rs_ssem.at[k], recv_sem=rs_rsem.at[k],
            device_id=(peer(j), z), device_id_type=MESH,
        )

    def stage_b(k):
        pair_copy(k).wait()
        for m in range(4):
            both = acc[core, m] + pair_recv[k, m * 256:(m + 1) * 256, :].astype(F32)
            rs_send[k, m * 256:(m + 1) * 256, :] = both.astype(BF)

        for j in FAR_FIRST:
            rs_copy(k, j).start()

    def own_rows():
        return pl.ds(pl.multiple_of(core * HALF + chip * OWN, OWN), OWN)

    def ag_copy(k, j):
        piece = res_v.at[k, own_rows(), :]
        return pltpu.make_async_remote_copy(
            src_ref=piece, dst_ref=piece,
            send_sem=ag_ssem.at[k], recv_sem=ag_rsem.at[k],
            device_id=(peer(j), z), device_id_type=MESH,
        )

    def all_bytes(k, sem):
        return pltpu.make_async_copy(rs_recv.at[k], rs_recv.at[k], sem.at[k])

    def stage_c(k):
        all_bytes(k, rs_rsem).wait()
        total = rs_send[k, pl.ds(pl.multiple_of(chip * OWN, OWN), OWN), :].astype(F32)
        for j in range(CHIPS - 1):
            total += rs_recv[k, j].astype(F32)
        left = ro_v[:, k * CW:(k + 1) * CW].astype(F32) - total
        res_v[k, own_rows(), :] = left.astype(BF)

        for j in FAR_FIRST:
            ag_copy(k, j).start()

    def sib_copy(k):
        piece = res_v.at[k, pl.ds(pl.multiple_of(core * HALF, HALF), HALF), :]
        return pltpu.make_async_remote_copy(
            src_ref=piece, dst_ref=piece,
            send_sem=sib_ssem.at[k], recv_sem=sib_rsem.at[k],
            device_id=(sibling, z), device_id_type=MESH,
        )

    def stage_d(k):
        all_bytes(k, ag_rsem).wait()
        sib_copy(k).start()

    def stage_e(k):
        sib_copy(k).wait()
        cols = slice(k * CW, (k + 1) * CW)
        for m in range(4):
            top = res_v[k, m * 256:(m + 1) * 256, :]
            low = res_v[k, HALF + m * 256:HALF + (m + 1) * 256, :]
            one_v[m, :256, cols] = jnp.dot(
                inv_one_v[m, :256, :256], top, preferred_element_type=F32
            ).astype(BF)
            one_v[m, 256:, cols] = (
                jnp.dot(inv_one_v[m, 256:, :256], top, preferred_element_type=F32)
                + jnp.dot(inv_one_v[m, 256:, 256:], low, preferred_element_type=F32)
            ).astype(BF)

    cp_inv.wait()
    cp_right.wait()
    own_panel(0)
    pl.semaphore_wait(barrier, CHIPS + 2)
    def loaded():
        cp_blocks.wait()
        for copy in lists:
            copy.wait()
        cp_ro.wait()
        cp_inv_one.wait()

    schedule = (
        (z_step(0, 0),),
        ([functools.partial(own_panel, 1)],),
        (z_step(1, 0),),
        ([functools.partial(own_panel, 2)],),
        ([functools.partial(own_panel, 3)],),
        ([loaded],),
        (z_step(0, 1),),
        (z_step(1, 1),),
        (z_step(0, 2),),
        (z_step(0, 3),),
        (z_step(2, 0),),
        (z_step(1, 2),),
        ([functools.partial(z_final, 0)],),
        (stage_a(0),),
        (z_step(2, 1),),
        ([functools.partial(stage_b, 0)],),
        (z_step(1, 3),),
        (z_step(2, 2),),
        (z_step(3, 0),),
        ([functools.partial(z_final, 1)],),
        (stage_a(1),),
        (z_step(2, 3),),
        ([functools.partial(stage_c, 0)],),
        ([functools.partial(stage_b, 1)],),
        (z_step(3, 1),),
        ([functools.partial(z_final, 2)],),
        (stage_a(2), z_step(3, 2),),
        ([functools.partial(stage_b, 2)],),
        ([functools.partial(stage_d, 0)],),
        (z_step(3, 3),),
        ([functools.partial(stage_c, 1)],),
        ([functools.partial(stage_e, 0)],),
        ([functools.partial(z_final, 3)],),
        (stage_a(3),),
        ([functools.partial(stage_b, 3)],),
        ([functools.partial(stage_c, 2)],),
        ([functools.partial(stage_d, 1)],),
        ([functools.partial(stage_c, 3)],),
        ([functools.partial(stage_e, 1)],),
        ([functools.partial(stage_d, 2)],),
        ([functools.partial(stage_e, 2)],),
        ([functools.partial(stage_d, 3)],),
        ([functools.partial(stage_e, 3)],),
    )
    for phase in schedule:
        longest = max(len(steps) for steps in phase)
        for i in range(longest):
            for steps in phase:
                for step in steps[i * len(steps) // longest:(i + 1) * len(steps) // longest]:
                    step()

    for k in range(NCH):
        piece = panels[k].at[0:7]
        pltpu.make_async_copy(piece, piece, z_send.at[k]).wait()
        all_bytes(k, rs_ssem).wait()
        all_bytes(k, ag_ssem).wait()


def body(
    right_zero, inverse_zero, factor_blocks, block_rows, block_cols, block_count, right_one, inverse_one,
):
    hbm = pl.BlockSpec(memory_space=pl.ANY)
    vm = pl.BlockSpec(memory_space=pltpu.VMEM)
    dma = pltpu.SemaphoreType.DMA
    one, zero = pl.pallas_call(
        fused,
        out_shape=(
            jax.ShapeDtypeStruct((4, W, W), BF),
            jax.ShapeDtypeStruct((W, W), BF),
        ),
        in_specs=[hbm, hbm, hbm, hbm, hbm, hbm, hbm, hbm],
        out_specs=(vm, vm),
        scratch_shapes=[
            pltpu.SMEM((6,), jnp.int32),
            pltpu.SMEM((6,), jnp.int32),
            pltpu.SMEM((1,), jnp.int32),
            pltpu.VMEM((W, W), BF),
            pltpu.VMEM((W, W), BF),
            pltpu.VMEM((6, W, W), BF),
            pltpu.VMEM((OWN, W), BF),
            pltpu.VMEM((4, W, W), BF),
            pltpu.VMEM((2, 4, 256, CW), F32),
        ]
        + [pltpu.VMEM((NZ, W, CW), BF)] * NCH
        + [
            pltpu.VMEM((NCH, HALF, CW), BF),
            pltpu.VMEM((NCH, HALF, CW), BF),
            pltpu.VMEM((NCH, HALF, CW), BF),
            pltpu.VMEM((NCH, CHIPS - 1, OWN, CW), BF),
            pltpu.VMEM((NCH, 4 * W, CW), BF),
            dma((8,)),
            dma((NCH,)),
            dma((NCH, 2, 4, 4)),
            dma((NCH,)), dma((NCH,)),
            dma((NCH,)), dma((NCH,)),
            dma((NCH,)), dma((NCH,)),
            dma((NCH,)), dma((NCH,)),
        ],
        compiler_params=pltpu.CompilerParams(
            collective_id=0, has_side_effects=True, vmem_limit_bytes=40 * 1024 * 1024
        ),
    )(
        pltpu.with_memory_space_constraint(block_rows[0, 0], pltpu.HBM),
        pltpu.with_memory_space_constraint(block_cols[0, 0], pltpu.HBM),
        block_count[0],
        *(
            pltpu.with_memory_space_constraint(operand, pltpu.HBM)
            for operand in (
                inverse_zero[0, 0, 0], right_zero[0, 0, 0],
                factor_blocks[0, 0], right_one[0], inverse_one[0],
            )
        ),
    )
    return (zero[None, None, None], one[None])


def solution(mesh):
    in_specs = (
        P("prow", "pcol", None, None, None),
        P("prow", "pcol", None, None, None),
        P("prow", "pcol", None, None, None),
        P("prow", "pcol", None),
        P("prow", "pcol", None),
        P("prow", "pcol"),
        P("pcol", None, None, None),
        P("pcol", None, None, None),
    )
    out_specs = (P("prow", "pcol", None, None, None), P("pcol", None, None, None))
    return jax.shard_map(body, mesh=mesh, in_specs=in_specs, out_specs=out_specs, check_vma=False)
```
